32 devices in a mesh: frame: 8 (over z, y), row: 4 (over x, core).
Axes of the slice: x: 2, y: 2, z: 4, core: 2. Of those that a mesh axis runs over, the one named last changes fastest.
Arguments:
- frames_x: bfloat16 [8, 24, 128, 512], P('frame', 'row'), may hold values from -6 to 6
- conv_weight: bfloat16 [3, 3, 512, 512], replicated, may hold values from -0.09375 to 0.09375
- conv_bias: float32 [512], replicated, may hold values from -3 to 3
- query_weight: bfloat16 [512, 512], replicated, may hold values from -0.25 to 0.25
- key_weight: bfloat16 [512, 512], replicated, may hold values from -0.25 to 0.25
- value_weight: bfloat16 [512, 512], replicated, may hold values from -0.25 to 0.25
- out_weight: bfloat16 [512, 512], replicated, may hold values from -0.25 to 0.25
- query_gain: float32 [512], replicated, may hold values from 0.5 to 2
- key_gain: float32 [512], replicated, may hold values from 0.5 to 2
- source_ids: int32 [8, 24, 4], P('frame', 'row'), may hold values from 0 to 23, as said below
- valid_counts: int32 [8, 24], P('frame', 'row'), may hold values from 1 to 4
Outputs:
- propagated: bfloat16 [8, 24, 128, 512], P('frame', 'row')
The draws below stay inside these ranges and needn't reach their ends.
Inputs may be any that keep to these rules, and one draw needn't show every extreme that they name: `source_ids`: block id s names row s // 1 of the previous frame, which lies at most 2 rows from the querying block's row; in every frame slot 0 of the blocks in even rows names a block 2 rows above and in odd rows 2 rows below, as far as the frame has that row.
All inputs are finite; a program needn't handle non-finite values.
Results may differ from the reference program's by a relative error of at most 0.0054.
Values may be sent and summed in bfloat16 or wider, within the bound.
A program may use at most 64 MiB of HBM per device.

```python
import math
import jax
import jax.numpy as jnp
from jax import lax

HEADS = 8
HD = 64
C = 512
KSRC = 4
BLOCK = 128
DISP = 2
W = 128
FRAMES = 8
H = 24
BPR = 1
NB = 24


def draw_source_ids(key, part):
    first_key, second_key = jax.random.split(jax.random.fold_in(key, 11))
    block_rows = jnp.arange(NB, dtype=jnp.int32) // BPR
    offsets = jax.random.randint(first_key, (FRAMES, NB, KSRC - 1), -DISP, DISP + 1)
    leading = jnp.where(block_rows % 2 == 0, -DISP, DISP).astype(jnp.int32)
    leading = jnp.broadcast_to(leading[None, :, None], (FRAMES, NB, 1))
    offsets = jnp.concatenate([leading, offsets.astype(jnp.int32)], axis=2)
    source_rows = jnp.clip(block_rows[None, :, None] + offsets, 0, H - 1)
    columns = jax.random.randint(second_key, (FRAMES, NB, KSRC), 0, BPR)
    return (source_rows * BPR + columns).astype(jnp.int32)


def plant(drawn, own_key, low, high):
    longest = drawn.shape.index(max(drawn.shape))
    spots = []
    for shift in (0, 1):
        where = [jax.random.randint(jax.random.fold_in(own_key, axis), (), 0, length) for axis, length in enumerate(drawn.shape)]
        where[longest] = (where[longest] + shift) % drawn.shape[longest]
        spots.append(tuple(where))
    return drawn.at[spots[0]].set(low).at[spots[1]].set(high)


def block_scale(stream_key, shape, shards, smallest, high):
    def one(position, blocks):
        draws = jax.random.uniform(jax.random.fold_in(jax.random.fold_in(stream_key, 6), position), (blocks,), jnp.float32, smallest / len(shards), high / len(shards))
        return jnp.repeat(jnp.exp(draws), shape[position] // blocks).reshape((-1,) + (1,) * (len(shape) - position - 1))

    factor_of = one(*shards[0])
    for cut in shards[1:]:
        factor_of = factor_of * one(*cut)
    return factor_of


def centred(own_key, extent, deviation, most, pieces=(), kind=jnp.bfloat16):
    array = deviation * jax.random.normal(own_key, extent, jnp.float32)
    if pieces:
        array = array * block_scale(own_key, extent, pieces, -0.22, 0.18)
    return jnp.clip(array, -most, most).astype(kind)


def setup_inputs(seed: int = 0) -> dict:
    streams_of = jax.random.split(jax.random.key(seed), 12)
    return {
        "frames_x": centred(streams_of[0], (FRAMES, H, W, C), 1.0, 6.0, ((0, 8), (1, 4))),
        "conv_weight": centred(streams_of[1], (3, 3, C, C), (9 * C) ** -0.5, 0.09375),
        "conv_bias": centred(streams_of[2], (C,), 0.5, 3.0, (), jnp.float32),
        "query_weight": centred(streams_of[3], (C, C), C ** -0.5, 0.25),
        "key_weight": centred(streams_of[4], (C, C), C ** -0.5, 0.25),
        "value_weight": centred(streams_of[5], (C, C), C ** -0.5, 0.25),
        "out_weight": centred(streams_of[6], (C, C), C ** -0.5, 0.25),
        "query_gain": jnp.clip(jnp.exp(jax.random.uniform(streams_of[7], (C,), jnp.float32, math.log(0.5), math.log(2.0))), 0.5, 2.0),
        "key_gain": jnp.clip(jnp.exp(jax.random.uniform(streams_of[8], (C,), jnp.float32, math.log(0.5), math.log(2.0))), 0.5, 2.0),
        "source_ids": draw_source_ids(jax.random.fold_in(streams_of[11], 71), 0),
        "valid_counts": plant(jax.random.randint(streams_of[10], (FRAMES, NB), 1, 5), jax.random.fold_in(streams_of[10], 1), 1, 4).astype(jnp.int32),
    }


def conv_frame(frame_in, conv_weight, conv_bias):
    padded = jnp.pad(frame_in, ((1, 1), (1, 1), (0, 0)))
    total = jnp.zeros((H * W, C), jnp.float32)
    for row_off in range(3):
        for col_off in range(3):
            window = padded[row_off:row_off + H, col_off:col_off + W].reshape(H * W, C)
            total = total + jnp.dot(window, conv_weight[row_off, col_off], preferred_element_type=jnp.float32)
    return (total + conv_bias).astype(jnp.bfloat16)

def normed(feats, weight, gain):
    proj = jnp.dot(feats, weight, preferred_element_type=jnp.float32).reshape(-1, HEADS, HD)
    proj = proj * lax.rsqrt(lax.optimization_barrier(jnp.mean(proj * proj, axis=-1, keepdims=True)) + 1e-06) * gain.reshape(HEADS, HD)
    return proj.reshape(-1, C).astype(jnp.bfloat16)

def attend(queries, key_set, value_set, mask):
    count = queries.shape[0]
    query_heads = queries.reshape(count, BLOCK, HEADS, HD).astype(jnp.float32)
    key_heads = key_set.reshape(count, -1, HEADS, HD).astype(jnp.float32)
    value_heads = value_set.reshape(count, -1, HEADS, HD).astype(jnp.float32)
    scores = jnp.einsum('nqhd,nkhd->nhqk', query_heads, key_heads) * HD ** (-0.5)
    expo = jnp.where(mask[:, None, None, :], jnp.exp(scores), 0.0)
    probs = (expo / lax.optimization_barrier(jnp.sum(expo, axis=-1, keepdims=True))).astype(jnp.bfloat16)
    mixed = jnp.einsum('nhqk,nkhd->nqhd', probs.astype(jnp.float32), value_heads)
    return mixed.reshape(count * BLOCK, C).astype(jnp.bfloat16)

def reference(frames_x, conv_weight, conv_bias, query_weight, key_weight, value_weight, out_weight, query_gain, key_gain, source_ids, valid_counts):
    feats_all = lax.map(lambda one: conv_frame(one, conv_weight, conv_bias), frames_x)
    queries_all = lax.map(lambda one: normed(one, query_weight, query_gain), feats_all)
    keys_all = lax.map(lambda one: normed(one, key_weight, key_gain), feats_all)
    values_all = lax.map(lambda one: jnp.dot(one, value_weight, preferred_element_type=jnp.float32).astype(jnp.bfloat16), feats_all)

    def one_frame(frame_pos):
        earlier = jnp.maximum(frame_pos - 1, 0)
        prev_keys = keys_all[earlier].reshape(NB, BLOCK, C)
        prev_values = values_all[earlier].reshape(NB, BLOCK, C)
        chosen = source_ids[frame_pos]
        key_set = jnp.concatenate([keys_all[frame_pos].reshape(NB, 1, BLOCK, C), prev_keys[chosen]], axis=1).reshape(NB, -1, C)
        value_set = jnp.concatenate([values_all[frame_pos].reshape(NB, 1, BLOCK, C), prev_values[chosen]], axis=1).reshape(NB, -1, C)
        slots = (jnp.arange(KSRC, dtype=jnp.int32)[None, :] < valid_counts[frame_pos][:, None]) & (frame_pos > 0)
        slot_mask = jnp.concatenate([jnp.ones((NB, 1), dtype=bool), slots], axis=1)
        mask = jnp.repeat(slot_mask, BLOCK, axis=1)
        mixed = attend(queries_all[frame_pos].reshape(NB, BLOCK, C), key_set, value_set, mask)
        result = feats_all[frame_pos].astype(jnp.float32) + jnp.dot(mixed, out_weight, preferred_element_type=jnp.float32)
        return result.astype(jnp.bfloat16).reshape(H, W, C)
    return lax.map(one_frame, jnp.arange(FRAMES, dtype=jnp.int32))
```

```python
import functools

import jax
import jax.numpy as jnp
from jax import lax
from jax.experimental import pallas as pl
from jax.experimental.pallas import tpu as pltpu
from jax.sharding import PartitionSpec as P

HEADS = 8
HD = 64
KSRC = 4
DISP = 2
GROUP = 4
F32 = jnp.float32
BF16 = jnp.bfloat16


def dot(a, b):
    return jnp.dot(a, b, preferred_element_type=F32)


def shift_columns(left, mid, right, width):
    count = mid.shape[0]
    col = lax.broadcasted_iota(jnp.int32, mid.shape, 0) % width
    return (
        mid
        + jnp.where(col == 0, 0.0, pltpu.roll(left, 1, 0))
        + jnp.where(col == width - 1, 0.0, pltpu.roll(right, count - 1, 0))
    )


def head_mean(chans):
    row = lax.broadcasted_iota(jnp.int32, (chans, chans), 0) // HD
    col = lax.broadcasted_iota(jnp.int32, (chans, chans), 1) // HD
    return jnp.where(row == col, 1.0 / HD, 0.0).astype(BF16)


def normed(feats, weight, gain, mean, scale):
    proj = dot(feats, weight)
    square = dot((proj * proj).astype(BF16), mean)
    out = (proj * lax.rsqrt(square + 1e-06) * gain).astype(BF16)
    return out * scale if scale != 1 else out


def conv_kernel(top, mid, bottom, weight, bias, feats, ext, left, centre, right):
    tap = pl.program_id(0)
    rows, width, chans = mid.shape
    count = rows * width

    @pl.when(tap == 0)
    def _():
        ext[0:width] = top[0]
        ext[width : width + count] = mid[...].reshape(count, chans)
        ext[width + count :] = bottom[0]

    window = ext[pl.ds(pl.multiple_of(tap * width, width), count)]
    for which, acc in enumerate((left, centre, right)):
        part = dot(window, weight[0, which])

        @pl.when(tap == 0)
        def _():
            acc[...] = part

        @pl.when(tap > 0)
        def _():
            acc[...] += part

    @pl.when(tap == 2)
    def _():
        total = shift_columns(left[...], centre[...], right[...], width)
        feats[...] = (total + bias[...]).astype(BF16)


def own_kernel(feats, wq, wk, wv, gq, gk, q, k, v):
    mean = head_mean(feats.shape[1])
    f = feats[...]
    q[...] = normed(f, wq[...], gq[...], mean, HD**-0.5)
    k[...] = normed(f, wk[...], gk[...], mean, 1)
    v[...] = dot(f, wv[...]).astype(BF16)


def attend_kernel(ids, valid, feats, q, k, v, above, prev, below, wk, wv, wo, gk, out, keys, values, mixed):
    nblocks, width, chans = q.shape
    mean = head_mean(chans)
    keys[0:nblocks] = k[...]
    values[0:nblocks] = v[...]
    at = nblocks
    for part in (above, prev, below):
        rows = part.shape[0]
        f = part[...].reshape(rows * width, chans)
        keys[at : at + rows] = normed(f, wk[...], gk[...], mean, 1).reshape(rows, width, chans)
        values[at : at + rows] = dot(f, wv[...]).astype(BF16).reshape(rows, width, chans)
        at += rows
    lanes = GROUP * HD
    head = lax.broadcasted_iota(jnp.int32, (1, lanes), 1) // HD
    slot = lax.broadcasted_iota(jnp.int32, (1, (1 + KSRC) * width), 1) // width

    def block(n, carry):
        places = [n] + [nblocks + ids[n, j] for j in range(KSRC)]
        mask = slot <= valid[n]
        for g in range(chans // lanes):
            cut = pl.ds(g * lanes, lanes)
            key = jnp.concatenate([keys[p, :, cut] for p in places], axis=0)
            value = jnp.concatenate([values[p, :, cut] for p in places], axis=0)
            query = q[n, :, cut]
            stack = jnp.concatenate(
                [jnp.where(head == h, query, jnp.zeros_like(query)) for h in range(GROUP)], axis=0
            )
            scores = lax.dot_general(
                stack, key, (((1,), (1,)), ((), ())), preferred_element_type=F32
            )
            expo = jnp.where(mask, jnp.exp(scores), 0.0)
            total = jnp.sum(expo, axis=1, keepdims=True)
            part = dot(expo.astype(BF16), value) / total
            joined = part[0:width]
            for h in range(1, GROUP):
                joined = jnp.where(head == h, part[h * width : (h + 1) * width], joined)
            mixed[n, :, cut] = joined.astype(BF16)
        return carry

    lax.fori_loop(0, nblocks, block, 0)
    flat = mixed[...].reshape(nblocks * width, chans)
    f = feats[...].reshape(nblocks * width, chans).astype(F32)
    out[...] = (f + dot(flat, wo[...])).astype(BF16).reshape(nblocks, width, chans)


VM = pl.BlockSpec(memory_space=pltpu.VMEM)
SM = pl.BlockSpec(memory_space=pltpu.SMEM)
PARAMS = dict(vmem_limit_bytes=48 * 2**20)


def shape(*dims):
    return jax.ShapeDtypeStruct(dims, BF16)


def edges(block, width):
    peers = lax.axis_size("row")
    up = [(i, i + 1) for i in range(peers - 1)]
    down = [(i + 1, i) for i in range(peers - 1)]
    rows = block.shape[0]
    before = lax.ppermute(block[rows - width :], "row", up)
    after = lax.ppermute(block[:width], "row", down)
    return before, after


def shards(x, wc, bias, wq, wk, wv, wo, gq, gk, source_ids, valid_counts):
    x = x[0]
    rows, width, chans = x.shape
    count = rows * width
    gq, gk, bias = gq[None], gk[None], bias[None]
    top, bottom = edges(x, 1)
    feats = pl.pallas_call(
        conv_kernel,
        grid=(3,),
        out_shape=shape(count, chans),
        in_specs=[VM, VM, VM, pl.BlockSpec((1, 3, chans, chans), lambda a: (a, 0, 0, 0)), VM],
        out_specs=VM,
        scratch_shapes=[pltpu.VMEM((count + 2 * width, chans), BF16)]
        + [pltpu.VMEM((count, chans), F32)] * 3,
        compiler_params=pltpu.CompilerParams(**PARAMS),
    )(top, x, bottom, wc, bias)
    frames = lax.axis_size("frame")
    prev = lax.ppermute(
        feats.reshape(rows, width, chans), "frame", [(i, i + 1) for i in range(frames - 1)]
    )
    q, k, v = pl.pallas_call(
        own_kernel,
        out_shape=(shape(count, chans),) * 3,
        in_specs=[VM] * 6,
        out_specs=(VM,) * 3,
        compiler_params=pltpu.CompilerParams(**PARAMS),
        cost_estimate=pl.CostEstimate(
            flops=10 * count * chans * chans, bytes_accessed=8 * count * chans, transcendentals=0
        ),
    )(feats, wq, wk, wv, gq, gk)
    above, below = edges(prev, DISP)
    ids = source_ids[0] - (lax.axis_index("row") * rows - DISP)
    valid = jnp.where(lax.axis_index("frame") > 0, valid_counts[0], 0)
    blocked = (rows, width, chans)
    out = pl.pallas_call(
        attend_kernel,
        out_shape=shape(*blocked),
        in_specs=[SM, SM] + [VM] * 11,
        out_specs=VM,
        scratch_shapes=[pltpu.VMEM((2 * rows + 2 * DISP, width, chans), BF16)] * 2
        + [pltpu.VMEM(blocked, BF16)],
        compiler_params=pltpu.CompilerParams(**PARAMS),
    )(
        ids,
        valid,
        feats.reshape(blocked),
        q.reshape(blocked),
        k.reshape(blocked),
        v.reshape(blocked),
        above,
        prev,
        below,
        wk,
        wv,
        wo,
        gk,
    )
    return out[None]


def solution(mesh):
    return jax.shard_map(
        shards,
        mesh=mesh,
        in_specs=(P("frame", "row", None, None),)
        + (P(),) * 8
        + (P("frame", "row", None), P("frame", "row")),
        out_specs=P("frame", "row", None, None),
        check_vma=False,
    )
```

```python
import functools

import jax
import jax.numpy as jnp
from jax import lax
from jax.experimental import pallas as pl
from jax.experimental.pallas import tpu as pltpu
from jax.sharding import PartitionSpec as P

HEADS = 8
HD = 64
KSRC = 4
DISP = 2
GROUP = 4
F32 = jnp.float32
BF16 = jnp.bfloat16


def dot(a, b):
    return jnp.dot(a, b, preferred_element_type=F32)


def shift_columns(left, mid, right, width):
    count = mid.shape[0]
    col = lax.broadcasted_iota(jnp.int32, mid.shape, 0) % width
    return (
        mid
        + jnp.where(col == 0, 0.0, pltpu.roll(left, 1, 0))
        + jnp.where(col == width - 1, 0.0, pltpu.roll(right, count - 1, 0))
    )


def head_mean(chans):
    row = lax.broadcasted_iota(jnp.int32, (chans, chans), 0) // HD
    col = lax.broadcasted_iota(jnp.int32, (chans, chans), 1) // HD
    return jnp.where(row == col, 1.0 / HD, 0.0).astype(BF16)


def normed(feats, weight, gain, mean, scale):
    proj = dot(feats, weight)
    square = dot((proj * proj).astype(BF16), mean)
    out = (proj * lax.rsqrt(square + 1e-06) * gain).astype(BF16)
    return out * scale if scale != 1 else out


def kernel(
    ids, valid, x, wc_hbm, wq_hbm, wk_hbm, wv_hbm, wo_hbm, bias, gq, gk,
    out,
    ext, wc, wq, wk, wv, wo, feats, reach, q, keys, values, mixed,
    local_sem, send_sem, recv_sem,
):
    rows, width, chans = x.shape
    frame, band = lax.axis_index("frame"), lax.axis_index("row")
    frames, bands = lax.axis_size("frame"), lax.axis_size("row")
    has_prev, has_next = frame > 0, frame < frames - 1
    has_above, has_below = band > 0, band < bands - 1
    to_above, to_below, to_next = {"row": band - 1}, {"row": band + 1}, {"frame": frame + 1}

    def fetch(i, src, dst):
        return pltpu.make_async_copy(src, dst, local_sem.at[i])

    def send(i, src, dst, device):
        return pltpu.make_async_remote_copy(
            src_ref=src,
            dst_ref=dst,
            send_sem=send_sem.at[i],
            recv_sem=recv_sem.at[i],
            device_id=device,
            device_id_type=pl.DeviceIdType.MESH,
        )

    load_x = fetch(0, x, ext.at[pl.ds(1, rows)])
    load_x.start()
    taps = [fetch(1 + b, wc_hbm.at[:, b], wc.at[:, b]) for b in range(3)]
    mats = [
        fetch(4 + i, src, dst)
        for i, (src, dst) in enumerate(
            ((wq_hbm, wq), (wk_hbm, wk), (wv_hbm, wv), (wo_hbm, wo))
        )
    ]
    for copy in taps + mats:
        copy.start()

    barrier = pltpu.get_barrier_semaphore()
    met = 0
    for there, device in (
        (has_above, to_above),
        (has_below, to_below),
        (has_prev, {"frame": frame - 1}),
        (has_next, to_next),
    ):
        met = met + there.astype(jnp.int32)

        @pl.when(there)
        def _():
            pl.semaphore_signal(
                barrier, inc=1, device_id=device, device_id_type=pl.DeviceIdType.MESH
            )

    pl.semaphore_wait(barrier, met)

    halo_up = send(0, x.at[0], ext.at[rows + 1], to_above)
    halo_down = send(1, x.at[rows - 1], ext.at[0], to_below)

    @pl.when(has_above)
    def _():
        halo_up.start()

    @pl.when(has_below)
    def _():
        halo_down.start()

    blank = jnp.zeros((width, chans), BF16)

    @pl.when(band == 0)
    def _():
        ext[0] = blank
        for i in range(DISP):
            reach[i] = blank

    @pl.when(band == bands - 1)
    def _():
        ext[rows + 1] = blank
        for i in range(DISP):
            reach[DISP + rows + i] = blank

    @pl.when(frame == 0)
    def _():
        for i in range(rows + 2 * DISP):
            reach[i] = blank

    spans = ((0, DISP), (rows - DISP, DISP), (DISP, rows - 2 * DISP))
    moves = [
        send(
            2 + i,
            feats.at[pl.ds(start, size)],
            reach.at[pl.ds(DISP + start, size)],
            to_next,
        )
        for i, (start, size) in enumerate(spans)
    ]
    relay_up = send(5, reach.at[pl.ds(DISP, DISP)], reach.at[pl.ds(DISP + rows, DISP)], to_above)
    relay_down = send(6, reach.at[pl.ds(rows, DISP)], reach.at[pl.ds(0, DISP)], to_below)

    load_x.wait()
    for i, (start, size) in enumerate(spans):
        if i == 0:

            @pl.when(has_above)
            def _():
                halo_down.wait_recv()

        if i == 1:

            @pl.when(has_below)
            def _():
                halo_up.wait_recv()

        window = jnp.concatenate(
            [ext[start + a : start + a + size].reshape(size * width, chans) for a in range(3)],
            axis=1,
        )
        parts = []
        for b in range(3):
            if i == 0:
                taps[b].wait()
            parts.append(dot(window, jnp.concatenate([wc[a, b] for a in range(3)], axis=0)))
        total = shift_columns(*parts, width) + bias[...]
        feats[start : start + size] = total.astype(BF16).reshape(size, width, chans)

        @pl.when(has_next)
        def _():
            moves[i].start()

    mean = head_mean(chans)

    def project(src, start, size, place):
        f = src[start : start + size].reshape(size * width, chans)
        blocked = (size, width, chans)
        keys[place : place + size] = normed(f, wk[...], gk[...], mean, 1).reshape(blocked)
        values[place : place + size] = dot(f, wv[...]).astype(BF16).reshape(blocked)

    for copy in mats:
        copy.wait()
    flat = feats[...].reshape(rows * width, chans)
    q[...] = normed(flat, wq[...], gq[...], mean, HD**-0.5).reshape(rows, width, chans)
    project(feats, 0, rows, 0)

    @pl.when(has_prev)
    def _():
        moves[0].wait_recv()

    @pl.when(has_prev & has_above)
    def _():
        relay_up.start()

    project(reach, DISP, DISP, rows + DISP)

    @pl.when(has_prev)
    def _():
        moves[1].wait_recv()

    @pl.when(has_prev & has_below)
    def _():
        relay_down.start()

    project(reach, rows, DISP, 2 * rows)

    @pl.when(has_prev & has_above)
    def _():
        relay_down.wait_recv()

    project(reach, 0, DISP, rows)

    @pl.when(has_prev & has_below)
    def _():
        relay_up.wait_recv()

    project(reach, DISP + rows, DISP, 2 * rows + DISP)

    @pl.when(has_prev)
    def _():
        moves[2].wait_recv()

    project(reach, 2 * DISP, rows - 2 * DISP, rows + 2 * DISP)

    lanes = GROUP * HD
    head = lax.broadcasted_iota(jnp.int32, (1, lanes), 1) // HD
    slot = lax.broadcasted_iota(jnp.int32, (1, (1 + KSRC) * width), 1) // width
    base = band * rows - DISP - rows
    live = has_prev.astype(jnp.int32)

    def block(n, carry):
        places = [n] + [
            jnp.clip(ids[0, n, j] - base, rows, 2 * rows + 2 * DISP - 1) for j in range(KSRC)
        ]
        mask = slot <= valid[0, n] * live
        for g in range(chans // lanes):
            cut = pl.ds(g * lanes, lanes)
            key = jnp.concatenate([keys[p, :, cut] for p in places], axis=0)
            value = jnp.concatenate([values[p, :, cut] for p in places], axis=0)
            query = q[n, :, cut]
            stack = jnp.concatenate(
                [jnp.where(head == h, query, jnp.zeros_like(query)) for h in range(GROUP)], axis=0
            )
            scores = lax.dot_general(
                stack, key, (((1,), (1,)), ((), ())), preferred_element_type=F32
            )
            expo = jnp.where(mask, jnp.exp(scores), 0.0)
            total = jnp.sum(expo, axis=1, keepdims=True)
            part = dot(expo.astype(BF16), value) / total
            joined = part[0:width]
            for h in range(1, GROUP):
                joined = jnp.where(head == h, part[h * width : (h + 1) * width], joined)
            mixed[n, :, cut] = joined.astype(BF16)
        return carry

    lax.fori_loop(0, rows, block, 0)
    flat = mixed[...].reshape(rows * width, chans)
    f = feats[...].reshape(rows * width, chans).astype(F32)
    out[...] = (f + dot(flat, wo[...])).astype(BF16).reshape(rows, width, chans)

    @pl.when(has_above)
    def _():
        halo_up.wait_send()

    @pl.when(has_below)
    def _():
        halo_down.wait_send()

    for copy in moves:

        @pl.when(has_next)
        def _():
            copy.wait_send()

    @pl.when(has_prev & has_above)
    def _():
        relay_up.wait_send()

    @pl.when(has_prev & has_below)
    def _():
        relay_down.wait_send()


VM = pl.BlockSpec(memory_space=pltpu.VMEM)
SM = pl.BlockSpec(memory_space=pltpu.SMEM)
ANY = pl.BlockSpec(memory_space=pl.ANY)


def shards(x, wc, bias, wq, wk, wv, wo, gq, gk, source_ids, valid_counts):
    x = x[0]
    rows, width, chans = x.shape
    square = pltpu.VMEM((chans, chans), BF16)

    def stack(count):
        return pltpu.VMEM((count, width, chans), BF16)

    out = pl.pallas_call(
        kernel,
        out_shape=jax.ShapeDtypeStruct((rows, width, chans), BF16),
        in_specs=[SM, SM] + [ANY] * 6 + [VM] * 3,
        out_specs=VM,
        scratch_shapes=[
            stack(rows + 2),
            pltpu.VMEM(wc.shape, BF16),
            square,
            square,
            square,
            square,
            stack(rows),
            stack(rows + 2 * DISP),
            stack(rows),
            stack(2 * rows + 2 * DISP),
            stack(2 * rows + 2 * DISP),
            stack(rows),
            pltpu.SemaphoreType.DMA((8,)),
            pltpu.SemaphoreType.DMA((7,)),
            pltpu.SemaphoreType.DMA((7,)),
        ],
        compiler_params=pltpu.CompilerParams(
            vmem_limit_bytes=56 * 2**20, collective_id=0, has_side_effects=True
        ),
    )(source_ids, valid_counts, x, wc, wq, wk, wv, wo, bias[None], gq[None], gk[None])
    return out[None]


def solution(mesh):
    return jax.shard_map(
        shards,
        mesh=mesh,
        in_specs=(P("frame", "row", None, None),)
        + (P(),) * 8
        + (P("frame", "row", None), P("frame", "row")),
        out_specs=P("frame", "row", None, None),
        check_vma=False,
    )
```

```python
import functools

import jax
import jax.numpy as jnp
from jax import lax
from jax.experimental import pallas as pl
from jax.experimental.pallas import tpu as pltpu
from jax.sharding import PartitionSpec as P

HEADS = 8
HD = 64
KSRC = 4
DISP = 2
GROUP = 4
F32 = jnp.float32
BF16 = jnp.bfloat16


def dot(a, b):
    return jnp.dot(a, b, preferred_element_type=F32)


def shift_columns(left, mid, right, width):
    count = mid.shape[0]
    col = lax.broadcasted_iota(jnp.int32, mid.shape, 0) % width
    return (
        mid
        + jnp.where(col == 0, 0.0, pltpu.roll(left, 1, 0))
        + jnp.where(col == width - 1, 0.0, pltpu.roll(right, count - 1, 0))
    )


def head_mean(chans):
    row = lax.broadcasted_iota(jnp.int32, (chans, chans), 0) // HD
    col = lax.broadcasted_iota(jnp.int32, (chans, chans), 1) // HD
    return jnp.where(row == col, 1.0 / HD, 0.0).astype(BF16)


def normed(feats, weight, gain, mean, scale):
    proj = dot(feats, weight)
    square = dot((proj * proj).astype(BF16), mean)
    out = (proj * lax.rsqrt(square + 1e-06) * gain).astype(BF16)
    return out * scale if scale != 1 else out


def kernel(
    ids, valid, x, wc_hbm, wq_hbm, wk_hbm, wv_hbm, bias, gq, gk,
    feats, mixed,
    ext, wc, wq, wk, wv, reach, q, keys, values, mixture, sums,
    local_sem, send_sem, recv_sem,
):
    rows, width, chans = x.shape
    frame, band = lax.axis_index("frame"), lax.axis_index("row")
    frames, bands = lax.axis_size("frame"), lax.axis_size("row")
    has_prev, has_next = frame > 0, frame < frames - 1
    has_above, has_below = band > 0, band < bands - 1
    to_above, to_below, to_next = {"row": band - 1}, {"row": band + 1}, {"frame": frame + 1}

    def fetch(i, src, dst):
        return pltpu.make_async_copy(src, dst, local_sem.at[i])

    def send(i, src, dst, device):
        return pltpu.make_async_remote_copy(
            src_ref=src,
            dst_ref=dst,
            send_sem=send_sem.at[i],
            recv_sem=recv_sem.at[i],
            device_id=device,
            device_id_type=pl.DeviceIdType.MESH,
        )

    load_x = fetch(0, x, ext.at[pl.ds(1, rows)])
    load_x.start()
    taps = [fetch(1 + b, wc_hbm.at[:, b], wc.at[:, b]) for b in range(3)]
    mats = [
        fetch(4 + i, src, dst)
        for i, (src, dst) in enumerate(
            ((wq_hbm, wq), (wk_hbm, wk), (wv_hbm, wv))
        )
    ]
    for copy in taps + mats:
        copy.start()

    barrier = pltpu.get_barrier_semaphore()
    met = 0
    for there, device in (
        (has_above, to_above),
        (has_below, to_below),
        (has_prev, {"frame": frame - 1}),
        (has_next, to_next),
    ):
        met = met + there.astype(jnp.int32)

        @pl.when(there)
        def _():
            pl.semaphore_signal(
                barrier, inc=1, device_id=device, device_id_type=pl.DeviceIdType.MESH
            )

    pl.semaphore_wait(barrier, met)

    halo_up = send(0, x.at[0], ext.at[rows + 1], to_above)
    halo_down = send(1, x.at[rows - 1], ext.at[0], to_below)

    @pl.when(has_above)
    def _():
        halo_up.start()

    @pl.when(has_below)
    def _():
        halo_down.start()

    blank = jnp.zeros((width, chans), BF16)

    @pl.when(band == 0)
    def _():
        ext[0] = blank
        for i in range(DISP):
            reach[i] = blank

    @pl.when(band == bands - 1)
    def _():
        ext[rows + 1] = blank
        for i in range(DISP):
            reach[DISP + rows + i] = blank

    @pl.when(frame == 0)
    def _():
        for i in range(rows + 2 * DISP):
            reach[i] = blank

    spans = ((0, DISP), (rows - DISP, DISP), (DISP, rows - 2 * DISP))
    moves = [
        send(
            2 + i,
            feats.at[pl.ds(start, size)],
            reach.at[pl.ds(DISP + start, size)],
            to_next,
        )
        for i, (start, size) in enumerate(spans)
    ]
    relay_up = send(5, reach.at[pl.ds(DISP, DISP)], reach.at[pl.ds(DISP + rows, DISP)], to_above)
    relay_down = send(6, reach.at[pl.ds(rows, DISP)], reach.at[pl.ds(0, DISP)], to_below)

    load_x.wait()
    for i, (start, size) in enumerate(spans):
        if i == 0:

            @pl.when(has_above)
            def _():
                halo_down.wait_recv()

        if i == 1:

            @pl.when(has_below)
            def _():
                halo_up.wait_recv()

        window = jnp.concatenate(
            [ext[start + a : start + a + size].reshape(size * width, chans) for a in range(3)],
            axis=1,
        )
        parts = []
        for b in range(3):
            if i == 0:
                taps[b].wait()
            parts.append(dot(window, jnp.concatenate([wc[a, b] for a in range(3)], axis=0)))
        total = shift_columns(*parts, width) + bias[...]
        feats[start : start + size] = total.astype(BF16).reshape(size, width, chans)

        @pl.when(has_next)
        def _():
            moves[i].start()

    mean = head_mean(chans)

    def project(src, start, size, place):
        f = src[start : start + size].reshape(size * width, chans)
        blocked = (size, width, chans)
        keys[place : place + size] = normed(f, wk[...], gk[...], mean, 1).reshape(blocked)
        values[place : place + size] = dot(f, wv[...]).astype(BF16).reshape(blocked)

    lanes = GROUP * HD
    head = lax.broadcasted_iota(jnp.int32, (1, lanes), 1) // HD
    base = band * rows - DISP
    live = has_prev.astype(jnp.int32)

    def by_head(stacked):
        joined = stacked[0:width]
        for h in range(1, GROUP):
            joined = jnp.where(head == h, stacked[h * width : (h + 1) * width], joined)
        return joined

    def times(n, row):
        limit = valid[0, n] * live
        found = 0
        for j in range(KSRC):
            found += ((ids[0, j, n] - base == row) & (j < limit)).astype(jnp.int32)
        return found.astype(F32)

    def attend(first, last, place, size, row):
        which = lax.broadcasted_iota(jnp.int32, (1, size * width), 1) // width

        def block(n, carry):
            if row is not None:
                weight = jnp.zeros((1, size * width), F32)
                for i in range(size):
                    weight = jnp.where(which == i, times(n, row + i), weight)
            for g in range(chans // lanes):
                cut = pl.ds(g * lanes, lanes)
                spot = pl.ds(n if row is None else place, size)
                key = keys[spot, :, cut].reshape(size * width, lanes)
                value = values[spot, :, cut].reshape(size * width, lanes)
                query = q[n, :, cut]
                stack = jnp.concatenate(
                    [jnp.where(head == h, query, jnp.zeros_like(query)) for h in range(GROUP)],
                    axis=0,
                )
                scores = lax.dot_general(
                    stack, key, (((1,), (1,)), ((), ())), preferred_element_type=F32
                )
                expo = jnp.exp(scores)
                if row is not None:
                    expo = expo * weight
                folded = expo[:, 0:width]
                for i in range(1, size):
                    folded = folded + expo[:, i * width : (i + 1) * width]
                part = by_head(dot(expo.astype(BF16), value))
                if row is None:
                    sums[n, g] = folded
                    mixture[n, :, cut] = part
                else:
                    sums[n, g] += folded
                    mixture[n, :, cut] += part
            return carry

        lax.fori_loop(first, last, block, 0)

    def meet(start, size):
        project(reach, start, size, rows + start)
        first = max(0, start - 2 * DISP)
        last = min(rows, start + size)
        attend(first, last, rows + start, size, start)

    for copy in mats:
        copy.wait()
    flat = feats[...].reshape(rows * width, chans)
    q[...] = normed(flat, wq[...], gq[...], mean, HD**-0.5).reshape(rows, width, chans)
    project(feats, 0, rows, 0)
    attend(0, rows, None, 1, None)

    @pl.when(has_prev)
    def _():
        moves[0].wait_recv()

    @pl.when(has_prev & has_above)
    def _():
        relay_up.start()

    meet(DISP, DISP)

    @pl.when(has_prev)
    def _():
        moves[1].wait_recv()

    @pl.when(has_prev & has_below)
    def _():
        relay_down.start()

    meet(rows, DISP)

    @pl.when(has_prev & has_above)
    def _():
        relay_down.wait_recv()

    meet(0, DISP)

    @pl.when(has_prev & has_below)
    def _():
        relay_up.wait_recv()

    meet(DISP + rows, DISP)

    @pl.when(has_prev)
    def _():
        moves[2].wait_recv()

    meet(2 * DISP, rows - 2 * DISP)

    def finish(n, carry):
        for g in range(chans // lanes):
            cut = pl.ds(g * lanes, lanes)
            inverse = 1.0 / jnp.sum(sums[n, g], axis=1, keepdims=True)
            mixed[n, :, cut] = (mixture[n, :, cut] * by_head(inverse)).astype(BF16)
        return carry

    lax.fori_loop(0, rows, finish, 0)

    @pl.when(has_above)
    def _():
        halo_up.wait_send()

    @pl.when(has_below)
    def _():
        halo_down.wait_send()

    for copy in moves:

        @pl.when(has_next)
        def _():
            copy.wait_send()

    @pl.when(has_prev & has_above)
    def _():
        relay_up.wait_send()

    @pl.when(has_prev & has_below)
    def _():
        relay_down.wait_send()


VM = pl.BlockSpec(memory_space=pltpu.VMEM)
SM = pl.BlockSpec(memory_space=pltpu.SMEM)
ANY = pl.BlockSpec(memory_space=pl.ANY)


def shards(x, wc, bias, wq, wk, wv, wo, gq, gk, source_ids, valid_counts):
    x = x[0]
    rows, width, chans = x.shape
    square = pltpu.VMEM((chans, chans), BF16)

    def stack(count):
        return pltpu.VMEM((count, width, chans), BF16)

    block = jax.ShapeDtypeStruct((rows, width, chans), BF16)
    feats, mixed = pl.pallas_call(
        kernel,
        out_shape=(block, block),
        in_specs=[SM, SM] + [ANY] * 5 + [VM] * 3,
        out_specs=(VM, VM),
        scratch_shapes=[
            stack(rows + 2),
            pltpu.VMEM(wc.shape, BF16),
            square,
            square,
            square,
            stack(rows + 2 * DISP),
            stack(rows),
            stack(2 * rows + 2 * DISP),
            stack(2 * rows + 2 * DISP),
            pltpu.VMEM((rows, width, chans), F32),
            pltpu.VMEM((rows, chans // (GROUP * HD), GROUP * width, width), F32),
            pltpu.SemaphoreType.DMA((8,)),
            pltpu.SemaphoreType.DMA((7,)),
            pltpu.SemaphoreType.DMA((7,)),
        ],
        compiler_params=pltpu.CompilerParams(
            vmem_limit_bytes=56 * 2**20, collective_id=0, has_side_effects=True
        ),
    )(jnp.swapaxes(source_ids, 1, 2), valid_counts, x, wc, wq, wk, wv, bias[None], gq[None], gk[None])
    mixed, feats = mixed.reshape(rows * width, chans), feats.reshape(rows * width, chans)
    out = (feats.astype(F32) + dot(mixed, wo)).astype(BF16)
    return out.reshape(1, rows, width, chans)


def solution(mesh):
    return jax.shard_map(
        shards,
        mesh=mesh,
        in_specs=(P("frame", "row", None, None),)
        + (P(),) * 8
        + (P("frame", "row", None), P("frame", "row")),
        out_specs=P("frame", "row", None, None),
        check_vma=False,
    )
```

```python
import functools

import jax
import jax.numpy as jnp
from jax import lax
from jax.experimental import pallas as pl
from jax.experimental.pallas import tpu as pltpu
from jax.sharding import PartitionSpec as P

HEADS = 8
HD = 64
KSRC = 4
DISP = 2
GROUP = 4
F32 = jnp.float32
BF16 = jnp.bfloat16


def dot(a, b):
    return jnp.dot(a, b, preferred_element_type=F32)


def shift_columns(left, mid, right, width):
    count = mid.shape[0]
    col = lax.broadcasted_iota(jnp.int32, mid.shape, 0) % width
    return (
        mid
        + jnp.where(col == 0, 0.0, pltpu.roll(left, 1, 0))
        + jnp.where(col == width - 1, 0.0, pltpu.roll(right, count - 1, 0))
    )


def head_mean(chans):
    row = lax.broadcasted_iota(jnp.int32, (chans, chans), 0) // HD
    col = lax.broadcasted_iota(jnp.int32, (chans, chans), 1) // HD
    return jnp.where(row == col, 1.0 / HD, 0.0).astype(BF16)


def normed(feats, weight, gain, mean, scale):
    proj = dot(feats, weight)
    square = dot((proj * proj).astype(BF16), mean)
    out = (proj * lax.rsqrt(square + 1e-06) * gain).astype(BF16)
    return out * scale if scale != 1 else out


def kernel(
    ids, valid, x, wc_hbm, wq_hbm, wk_hbm, wv_hbm, wo_hbm, bias, gq, gk,
    out,
    ext, wc, wq, wk, wv, wo, feats, reach, q, keys, values, mixed, mixture, sums,
    local_sem, send_sem, recv_sem,
):
    rows, width, chans = x.shape
    frame, band = lax.axis_index("frame"), lax.axis_index("row")
    frames, bands = lax.axis_size("frame"), lax.axis_size("row")
    has_prev, has_next = frame > 0, frame < frames - 1
    has_above, has_below = band > 0, band < bands - 1
    to_above, to_below, to_next = {"row": band - 1}, {"row": band + 1}, {"frame": frame + 1}

    def fetch(i, src, dst):
        return pltpu.make_async_copy(src, dst, local_sem.at[i])

    def send(i, src, dst, device):
        return pltpu.make_async_remote_copy(
            src_ref=src,
            dst_ref=dst,
            send_sem=send_sem.at[i],
            recv_sem=recv_sem.at[i],
            device_id=device,
            device_id_type=pl.DeviceIdType.MESH,
        )

    load_x = fetch(0, x, ext.at[pl.ds(1, rows)])
    load_x.start()
    taps = [fetch(1 + b, wc_hbm.at[:, b], wc.at[:, b]) for b in range(3)]
    mats = [
        fetch(4 + i, src, dst)
        for i, (src, dst) in enumerate(
            ((wq_hbm, wq), (wk_hbm, wk), (wv_hbm, wv), (wo_hbm, wo))
        )
    ]
    for copy in taps + mats:
        copy.start()

    barrier = pltpu.get_barrier_semaphore()
    met = 0
    for there, device in (
        (has_above, to_above),
        (has_below, to_below),
        (has_prev, {"frame": frame - 1}),
        (has_next, to_next),
    ):
        met = met + there.astype(jnp.int32)

        @pl.when(there)
        def _():
            pl.semaphore_signal(
                barrier, inc=1, device_id=device, device_id_type=pl.DeviceIdType.MESH
            )

    pl.semaphore_wait(barrier, met)

    halo_up = send(0, x.at[0], ext.at[rows + 1], to_above)
    halo_down = send(1, x.at[rows - 1], ext.at[0], to_below)

    @pl.when(has_above)
    def _():
        halo_up.start()

    @pl.when(has_below)
    def _():
        halo_down.start()

    blank = jnp.zeros((width, chans), BF16)

    @pl.when(band == 0)
    def _():
        ext[0] = blank
        for i in range(DISP):
            reach[i] = blank

    @pl.when(band == bands - 1)
    def _():
        ext[rows + 1] = blank
        for i in range(DISP):
            reach[DISP + rows + i] = blank

    @pl.when(frame == 0)
    def _():
        for i in range(rows + 2 * DISP):
            reach[i] = blank

    spans = ((0, DISP), (rows - DISP, DISP), (DISP, rows - 2 * DISP))
    moves = [
        send(
            2 + i,
            feats.at[pl.ds(start, size)],
            reach.at[pl.ds(DISP + start, size)],
            to_next,
        )
        for i, (start, size) in enumerate(spans)
    ]
    relay_up = send(5, reach.at[pl.ds(DISP, DISP)], reach.at[pl.ds(DISP + rows, DISP)], to_above)
    relay_down = send(6, reach.at[pl.ds(rows, DISP)], reach.at[pl.ds(0, DISP)], to_below)

    load_x.wait()
    for i, (start, size) in enumerate(spans):
        if i == 0:

            @pl.when(has_above)
            def _():
                halo_down.wait_recv()

        if i == 1:

            @pl.when(has_below)
            def _():
                halo_up.wait_recv()

        window = jnp.concatenate(
            [ext[start + a : start + a + size].reshape(size * width, chans) for a in range(3)],
            axis=1,
        )
        parts = []
        for b in range(3):
            if i == 0:
                taps[b].wait()
            parts.append(dot(window, jnp.concatenate([wc[a, b] for a in range(3)], axis=0)))
        total = shift_columns(*parts, width) + bias[...]
        feats[start : start + size] = total.astype(BF16).reshape(size, width, chans)

        @pl.when(has_next)
        def _():
            moves[i].start()

    mean = head_mean(chans)

    def project(src, start, size, place):
        f = src[start : start + size].reshape(size * width, chans)
        blocked = (size, width, chans)
        keys[place : place + size] = normed(f, wk[...], gk[...], mean, 1).reshape(blocked)
        values[place : place + size] = dot(f, wv[...]).astype(BF16).reshape(blocked)

    lanes = GROUP * HD
    head = lax.broadcasted_iota(jnp.int32, (1, lanes), 1) // HD
    slot = lax.broadcasted_iota(jnp.int32, (1, KSRC * width), 1) // width
    base = band * rows - DISP - rows
    live = has_prev.astype(jnp.int32)

    def by_head(stacked):
        joined = stacked[0:width]
        for h in range(1, GROUP):
            joined = jnp.where(head == h, stacked[h * width : (h + 1) * width], joined)
        return joined

    def exponentials(n, cut, key):
        query = q[n, :, cut]
        stack = jnp.concatenate(
            [jnp.where(head == h, query, jnp.zeros_like(query)) for h in range(GROUP)], axis=0
        )
        return jnp.exp(
            lax.dot_general(stack, key, (((1,), (1,)), ((), ())), preferred_element_type=F32)
        )

    def own(n, carry):
        for g in range(chans // lanes):
            cut = pl.ds(g * lanes, lanes)
            expo = exponentials(n, cut, keys[n, :, cut])
            sums[n, g] = expo
            mixture[n, :, cut] = by_head(dot(expo.astype(BF16), values[n, :, cut]))
        return carry

    def block(n, carry):
        places = [
            jnp.clip(ids[0, j, n] - base, rows, 2 * rows + 2 * DISP - 1) for j in range(KSRC)
        ]
        mask = slot < valid[0, n] * live
        for g in range(chans // lanes):
            cut = pl.ds(g * lanes, lanes)
            key = jnp.concatenate([keys[p, :, cut] for p in places], axis=0)
            value = jnp.concatenate([values[p, :, cut] for p in places], axis=0)
            expo = jnp.where(mask, exponentials(n, cut, key), 0.0)
            folded = sums[n, g]
            for j in range(KSRC):
                folded = folded + expo[:, j * width : (j + 1) * width]
            inverse = 1.0 / jnp.sum(folded, axis=1, keepdims=True)
            part = by_head(dot(expo.astype(BF16), value)) + mixture[n, :, cut]
            mixed[n, :, cut] = (part * by_head(inverse)).astype(BF16)
        return carry

    for copy in mats:
        copy.wait()
    flat = feats[...].reshape(rows * width, chans)
    q[...] = normed(flat, wq[...], gq[...], mean, HD**-0.5).reshape(rows, width, chans)
    project(feats, 0, rows, 0)

    @pl.when(has_prev)
    def _():
        moves[0].wait_recv()

    @pl.when(has_prev & has_above)
    def _():
        relay_up.start()

    project(reach, DISP, DISP, rows + DISP)
    lax.fori_loop(0, rows, own, 0)

    @pl.when(has_prev)
    def _():
        moves[1].wait_recv()

    @pl.when(has_prev & has_below)
    def _():
        relay_down.start()

    project(reach, rows, DISP, 2 * rows)

    @pl.when(has_prev & has_above)
    def _():
        relay_down.wait_recv()

    project(reach, 0, DISP, rows)

    @pl.when(has_prev & has_below)
    def _():
        relay_up.wait_recv()

    project(reach, DISP + rows, DISP, 2 * rows + DISP)

    @pl.when(has_prev)
    def _():
        moves[2].wait_recv()

    project(reach, 2 * DISP, rows - 2 * DISP, rows + 2 * DISP)

    lax.fori_loop(0, rows, block, 0)
    flat = mixed[...].reshape(rows * width, chans)
    f = feats[...].reshape(rows * width, chans).astype(F32)
    out[...] = (f + dot(flat, wo[...])).astype(BF16).reshape(rows, width, chans)

    @pl.when(has_above)
    def _():
        halo_up.wait_send()

    @pl.when(has_below)
    def _():
        halo_down.wait_send()

    for copy in moves:

        @pl.when(has_next)
        def _():
            copy.wait_send()

    @pl.when(has_prev & has_above)
    def _():
        relay_up.wait_send()

    @pl.when(has_prev & has_below)
    def _():
        relay_down.wait_send()


VM = pl.BlockSpec(memory_space=pltpu.VMEM)
SM = pl.BlockSpec(memory_space=pltpu.SMEM)
ANY = pl.BlockSpec(memory_space=pl.ANY)


def shards(x, wc, bias, wq, wk, wv, wo, gq, gk, source_ids, valid_counts):
    x = x[0]
    rows, width, chans = x.shape
    square = pltpu.VMEM((chans, chans), BF16)

    def stack(count):
        return pltpu.VMEM((count, width, chans), BF16)

    out = pl.pallas_call(
        kernel,
        out_shape=jax.ShapeDtypeStruct((rows, width, chans), BF16),
        in_specs=[SM, SM] + [ANY] * 6 + [VM] * 3,
        out_specs=VM,
        scratch_shapes=[
            stack(rows + 2),
            pltpu.VMEM(wc.shape, BF16),
            square,
            square,
            square,
            square,
            stack(rows),
            stack(rows + 2 * DISP),
            stack(rows),
            stack(2 * rows + 2 * DISP),
            stack(2 * rows + 2 * DISP),
            stack(rows),
            pltpu.VMEM((rows, width, chans), F32),
            pltpu.VMEM((rows, chans // (GROUP * HD), GROUP * width, width), F32),
            pltpu.SemaphoreType.DMA((8,)),
            pltpu.SemaphoreType.DMA((7,)),
            pltpu.SemaphoreType.DMA((7,)),
        ],
        compiler_params=pltpu.CompilerParams(
            vmem_limit_bytes=56 * 2**20, collective_id=0, has_side_effects=True
        ),
    )(jnp.swapaxes(source_ids, 1, 2), valid_counts, x, wc, wq, wk, wv, wo, bias[None], gq[None], gk[None])
    return out[None]


def solution(mesh):
    return jax.shard_map(
        shards,
        mesh=mesh,
        in_specs=(P("frame", "row", None, None),)
        + (P(),) * 8
        + (P("frame", "row", None), P("frame", "row")),
        out_specs=P("frame", "row", None, None),
        check_vma=False,
    )
```

```python
import functools

import jax
import jax.numpy as jnp
from jax import lax
from jax.experimental import pallas as pl
from jax.experimental.pallas import tpu as pltpu
from jax.sharding import PartitionSpec as P

HEADS = 8
HD = 64
KSRC = 4
DISP = 2
GROUP = 4
F32 = jnp.float32
BF16 = jnp.bfloat16


def dot(a, b):
    return jnp.dot(a, b, preferred_element_type=F32)


def shift_columns(left, mid, right, width):
    count = mid.shape[0]
    col = lax.broadcasted_iota(jnp.int32, mid.shape, 0) % width
    return (
        mid
        + jnp.where(col == 0, 0.0, pltpu.roll(left, 1, 0))
        + jnp.where(col == width - 1, 0.0, pltpu.roll(right, count - 1, 0))
    )


def head_mean(chans):
    row = lax.broadcasted_iota(jnp.int32, (chans, chans), 0) // HD
    col = lax.broadcasted_iota(jnp.int32, (chans, chans), 1) // HD
    return jnp.where(row == col, 1.0 / HD, 0.0).astype(BF16)


def normed(feats, weight, gain, mean, scale):
    proj = dot(feats, weight)
    square = dot((proj * proj).astype(BF16), mean)
    out = (proj * lax.rsqrt(square + 1e-06) * gain).astype(BF16)
    return out * scale if scale != 1 else out


def kernel(
    ids, valid, x, wc_hbm, wq_hbm, wk_hbm, wv_hbm, wo_hbm, bias, gq, gk,
    out,
    ext, wc, wq, wk, wv, wo, feats, reach, q, keys, values, mixed, mixture, sums,
    local_sem, send_sem, recv_sem,
):
    rows, width, chans = x.shape
    frame, band = lax.axis_index("frame"), lax.axis_index("row")
    frames, bands = lax.axis_size("frame"), lax.axis_size("row")
    has_prev, has_next = frame > 0, frame < frames - 1
    has_above, has_below = band > 0, band < bands - 1
    to_above, to_below, to_next = {"row": band - 1}, {"row": band + 1}, {"frame": frame + 1}

    def fetch(i, src, dst):
        return pltpu.make_async_copy(src, dst, local_sem.at[i])

    def send(i, src, dst, device):
        return pltpu.make_async_remote_copy(
            src_ref=src,
            dst_ref=dst,
            send_sem=send_sem.at[i],
            recv_sem=recv_sem.at[i],
            device_id=device,
            device_id_type=pl.DeviceIdType.MESH,
        )

    load_x = fetch(0, x, ext.at[pl.ds(1, rows)])
    load_x.start()
    taps = [fetch(1 + b, wc_hbm.at[:, b], wc.at[:, b]) for b in range(3)]
    mats = [
        fetch(4 + i, src, dst)
        for i, (src, dst) in enumerate(
            ((wq_hbm, wq), (wk_hbm, wk), (wv_hbm, wv), (wo_hbm, wo))
        )
    ]
    for copy in taps + mats:
        copy.start()

    barrier = pltpu.get_barrier_semaphore()
    met = 0
    for there, device in (
        (has_above, to_above),
        (has_below, to_below),
        (has_prev, {"frame": frame - 1}),
        (has_next, to_next),
    ):
        met = met + there.astype(jnp.int32)

        @pl.when(there)
        def _():
            pl.semaphore_signal(
                barrier, inc=1, device_id=device, device_id_type=pl.DeviceIdType.MESH
            )

    pl.semaphore_wait(barrier, met)

    halo_up = send(0, x.at[0], ext.at[rows + 1], to_above)
    halo_down = send(1, x.at[rows - 1], ext.at[0], to_below)

    @pl.when(has_above)
    def _():
        halo_up.start()

    @pl.when(has_below)
    def _():
        halo_down.start()

    blank = jnp.zeros((width, chans), BF16)

    @pl.when(band == 0)
    def _():
        ext[0] = blank
        for i in range(DISP):
            reach[i] = blank

    @pl.when(band == bands - 1)
    def _():
        ext[rows + 1] = blank
        for i in range(DISP):
            reach[DISP + rows + i] = blank

    @pl.when(frame == 0)
    def _():
        for i in range(rows + 2 * DISP):
            reach[i] = blank

    spans = ((0, DISP), (rows - DISP, DISP), (DISP, rows - 2 * DISP))
    moves = [
        send(
            2 + i,
            feats.at[pl.ds(start, size)],
            reach.at[pl.ds(DISP + start, size)],
            to_next,
        )
        for i, (start, size) in enumerate(spans)
    ]
    relay_up = send(5, reach.at[pl.ds(DISP, DISP)], reach.at[pl.ds(DISP + rows, DISP)], to_above)
    relay_down = send(6, reach.at[pl.ds(rows, DISP)], reach.at[pl.ds(0, DISP)], to_below)

    load_x.wait()
    for i, (start, size) in enumerate(spans):
        if i == 0:

            @pl.when(has_above)
            def _():
                halo_down.wait_recv()

        if i == 1:

            @pl.when(has_below)
            def _():
                halo_up.wait_recv()

        window = jnp.concatenate(
            [ext[start + a : start + a + size].reshape(size * width, chans) for a in range(3)],
            axis=1,
        )
        parts = []
        for b in range(3):
            if i == 0:
                taps[b].wait()
            parts.append(dot(window, jnp.concatenate([wc[a, b] for a in range(3)], axis=0)))
        total = shift_columns(*parts, width) + bias[...]
        feats[start : start + size] = total.astype(BF16).reshape(size, width, chans)

        @pl.when(has_next)
        def _():
            moves[i].start()

    mean = head_mean(chans)

    def project(src, start, size, place):
        f = src[start : start + size].reshape(size * width, chans)
        blocked = (size, width, chans)
        keys[place : place + size] = normed(f, wk[...], gk[...], mean, 1).reshape(blocked)
        values[place : place + size] = dot(f, wv[...]).astype(BF16).reshape(blocked)

    lanes = GROUP * HD
    head = lax.broadcasted_iota(jnp.int32, (1, lanes), 1) // HD
    slot = lax.broadcasted_iota(jnp.int32, (1, KSRC * width), 1) // width
    base = band * rows - DISP - rows
    live = has_prev.astype(jnp.int32)

    def by_head(stacked):
        joined = stacked[0:width]
        for h in range(1, GROUP):
            joined = jnp.where(head == h, stacked[h * width : (h + 1) * width], joined)
        return joined

    def exponentials(n, cut, key):
        query = q[n, :, cut]
        stack = jnp.concatenate(
            [jnp.where(head == h, query, jnp.zeros_like(query)) for h in range(GROUP)], axis=0
        )
        return jnp.exp(
            lax.dot_general(stack, key, (((1,), (1,)), ((), ())), preferred_element_type=F32)
        )

    def own(n, carry):
        for g in range(chans // lanes):
            cut = pl.ds(g * lanes, lanes)
            expo = exponentials(n, cut, keys[n, :, cut])
            sums[n, g] = expo
            mixture[n, :, cut] = by_head(dot(expo.astype(BF16), values[n, :, cut]))
        return carry

    def block(n, carry):
        places = [
            jnp.clip(ids[0, j, n] - base, rows, 2 * rows + 2 * DISP - 1) for j in range(KSRC)
        ]
        mask = slot < valid[0, n] * live
        for g in range(chans // lanes):
            cut = pl.ds(g * lanes, lanes)
            key = jnp.concatenate([keys[p, :, cut] for p in places], axis=0)
            value = jnp.concatenate([values[p, :, cut] for p in places], axis=0)
            expo = jnp.where(mask, exponentials(n, cut, key), 0.0)
            folded = sums[n, g]
            for j in range(KSRC):
                folded = folded + expo[:, j * width : (j + 1) * width]
            inverse = 1.0 / jnp.sum(folded, axis=1, keepdims=True)
            part = by_head(dot(expo.astype(BF16), value)) + mixture[n, :, cut]
            mixed[n, :, cut] = (part * by_head(inverse)).astype(BF16)
        return carry

    for copy in mats:
        copy.wait()
    flat = feats[...].reshape(rows * width, chans)
    q[...] = normed(flat, wq[...], gq[...], mean, HD**-0.5).reshape(rows, width, chans)
    project(feats, 0, rows, 0)

    @pl.when(has_prev)
    def _():
        moves[0].wait_recv()

    @pl.when(has_prev & has_above)
    def _():
        relay_up.start()

    project(reach, DISP, DISP, rows + DISP)
    lax.fori_loop(0, rows, own, 0, unroll=True)

    @pl.when(has_prev)
    def _():
        moves[1].wait_recv()

    @pl.when(has_prev & has_below)
    def _():
        relay_down.start()

    project(reach, rows, DISP, 2 * rows)

    @pl.when(has_prev & has_above)
    def _():
        relay_down.wait_recv()

    project(reach, 0, DISP, rows)

    @pl.when(has_prev & has_below)
    def _():
        relay_up.wait_recv()

    project(reach, DISP + rows, DISP, 2 * rows + DISP)

    @pl.when(has_prev)
    def _():
        moves[2].wait_recv()

    project(reach, 2 * DISP, rows - 2 * DISP, rows + 2 * DISP)

    lax.fori_loop(0, rows, block, 0, unroll=True)
    flat = mixed[...].reshape(rows * width, chans)
    f = feats[...].reshape(rows * width, chans).astype(F32)
    out[...] = (f + dot(flat, wo[...])).astype(BF16).reshape(rows, width, chans)

    @pl.when(has_above)
    def _():
        halo_up.wait_send()

    @pl.when(has_below)
    def _():
        halo_down.wait_send()

    for copy in moves:

        @pl.when(has_next)
        def _():
            copy.wait_send()

    @pl.when(has_prev & has_above)
    def _():
        relay_up.wait_send()

    @pl.when(has_prev & has_below)
    def _():
        relay_down.wait_send()


VM = pl.BlockSpec(memory_space=pltpu.VMEM)
SM = pl.BlockSpec(memory_space=pltpu.SMEM)
ANY = pl.BlockSpec(memory_space=pl.ANY)


def shards(x, wc, bias, wq, wk, wv, wo, gq, gk, source_ids, valid_counts):
    x = x[0]
    rows, width, chans = x.shape
    square = pltpu.VMEM((chans, chans), BF16)

    def stack(count):
        return pltpu.VMEM((count, width, chans), BF16)

    out = pl.pallas_call(
        kernel,
        out_shape=jax.ShapeDtypeStruct((rows, width, chans), BF16),
        in_specs=[SM, SM] + [ANY] * 6 + [VM] * 3,
        out_specs=VM,
        scratch_shapes=[
            stack(rows + 2),
            pltpu.VMEM(wc.shape, BF16),
            square,
            square,
            square,
            square,
            stack(rows),
            stack(rows + 2 * DISP),
            stack(rows),
            stack(2 * rows + 2 * DISP),
            stack(2 * rows + 2 * DISP),
            stack(rows),
            pltpu.VMEM((rows, width, chans), F32),
            pltpu.VMEM((rows, chans // (GROUP * HD), GROUP * width, width), F32),
            pltpu.SemaphoreType.DMA((8,)),
            pltpu.SemaphoreType.DMA((7,)),
            pltpu.SemaphoreType.DMA((7,)),
        ],
        compiler_params=pltpu.CompilerParams(
            vmem_limit_bytes=56 * 2**20, collective_id=0, has_side_effects=True
        ),
    )(jnp.swapaxes(source_ids, 1, 2), valid_counts, x, wc, wq, wk, wv, wo, bias[None], gq[None], gk[None])
    return out[None]


def solution(mesh):
    return jax.shard_map(
        shards,
        mesh=mesh,
        in_specs=(P("frame", "row", None, None),)
        + (P(),) * 8
        + (P("frame", "row", None), P("frame", "row")),
        out_specs=P("frame", "row", None, None),
        check_vma=False,
    )
```

```python
import functools

import jax
import jax.numpy as jnp
from jax import lax
from jax.experimental import pallas as pl
from jax.experimental.pallas import tpu as pltpu
from jax.sharding import PartitionSpec as P

HEADS = 8
HD = 64
KSRC = 4
DISP = 2
GROUP = 4
F32 = jnp.float32
BF16 = jnp.bfloat16


def dot(a, b):
    return jnp.dot(a, b, preferred_element_type=F32)


def shift_columns(left, mid, right, width):
    count = mid.shape[0]
    col = lax.broadcasted_iota(jnp.int32, mid.shape, 0) % width
    return (
        mid
        + jnp.where(col == 0, 0.0, pltpu.roll(left, 1, 0))
        + jnp.where(col == width - 1, 0.0, pltpu.roll(right, count - 1, 0))
    )


def head_mean(chans):
    row = lax.broadcasted_iota(jnp.int32, (chans, chans), 0) // HD
    col = lax.broadcasted_iota(jnp.int32, (chans, chans), 1) // HD
    return jnp.where(row == col, 1.0 / HD, 0.0).astype(BF16)


def normed(feats, weight, gain, mean, scale):
    proj = dot(feats, weight)
    square = dot((proj * proj).astype(BF16), mean)
    out = (proj * lax.rsqrt(square + 1e-06) * gain).astype(BF16)
    return out * scale if scale != 1 else out


def kernel(
    ids, valid, x, wc_hbm, wq_hbm, wk_hbm, wv_hbm, wo_hbm, bias, gq, gk,
    out,
    ext, wc, wq, wk, wv, wo, feats, reach, q, keys, values, mixed, mixture, sums,
    local_sem, send_sem, recv_sem,
):
    rows, width, chans = x.shape
    frame, band = lax.axis_index("frame"), lax.axis_index("row")
    frames, bands = lax.axis_size("frame"), lax.axis_size("row")
    has_prev, has_next = frame > 0, frame < frames - 1
    has_above, has_below = band > 0, band < bands - 1
    to_above, to_below, to_next = {"row": band - 1}, {"row": band + 1}, {"frame": frame + 1}

    def fetch(i, src, dst):
        return pltpu.make_async_copy(src, dst, local_sem.at[i])

    def send(i, src, dst, device):
        return pltpu.make_async_remote_copy(
            src_ref=src,
            dst_ref=dst,
            send_sem=send_sem.at[i],
            recv_sem=recv_sem.at[i],
            device_id=device,
            device_id_type=pl.DeviceIdType.MESH,
        )

    barrier = pltpu.get_barrier_semaphore()
    met = 0
    for there, device in (
        (has_above, to_above),
        (has_below, to_below),
        (has_prev, {"frame": frame - 1}),
        (has_next, to_next),
    ):
        met = met + there.astype(jnp.int32)

        @pl.when(there)
        def _():
            pl.semaphore_signal(
                barrier, inc=1, device_id=device, device_id_type=pl.DeviceIdType.MESH
            )

    load_x = fetch(0, x, ext.at[pl.ds(1, rows)])
    load_x.start()
    taps = [fetch(1 + b, wc_hbm.at[:, b], wc.at[:, b]) for b in range(3)]
    mats = [
        fetch(4 + i, src, dst)
        for i, (src, dst) in enumerate(
            ((wq_hbm, wq), (wk_hbm, wk), (wv_hbm, wv), (wo_hbm, wo))
        )
    ]
    for copy in taps:
        copy.start()

    pl.semaphore_wait(barrier, met)

    halo_up = send(0, x.at[0], ext.at[rows + 1], to_above)
    halo_down = send(1, x.at[rows - 1], ext.at[0], to_below)

    @pl.when(has_above)
    def _():
        halo_up.start()

    @pl.when(has_below)
    def _():
        halo_down.start()

    blank = jnp.zeros((width, chans), BF16)

    @pl.when(band == 0)
    def _():
        ext[0] = blank
        for i in range(DISP):
            reach[i] = blank

    @pl.when(band == bands - 1)
    def _():
        ext[rows + 1] = blank
        for i in range(DISP):
            reach[DISP + rows + i] = blank

    @pl.when(frame == 0)
    def _():
        for i in range(rows + 2 * DISP):
            reach[i] = blank

    spans = ((0, DISP), (rows - DISP, DISP), (DISP, rows - 2 * DISP))
    moves = [
        send(
            2 + i,
            feats.at[pl.ds(start, size)],
            reach.at[pl.ds(DISP + start, size)],
            to_next,
        )
        for i, (start, size) in enumerate(spans)
    ]
    relay_up = send(5, reach.at[pl.ds(DISP, DISP)], reach.at[pl.ds(DISP + rows, DISP)], to_above)
    relay_down = send(6, reach.at[pl.ds(rows, DISP)], reach.at[pl.ds(0, DISP)], to_below)

    load_x.wait()
    for i, (start, size) in enumerate(spans):
        if i == 0:

            @pl.when(has_above)
            def _():
                halo_down.wait_recv()

        if i == 1:

            @pl.when(has_below)
            def _():
                halo_up.wait_recv()

        window = jnp.concatenate(
            [ext[start + a : start + a + size].reshape(size * width, chans) for a in range(3)],
            axis=1,
        )
        parts = []
        for b in range(3):
            if i == 0:
                taps[b].wait()
            parts.append(dot(window, jnp.concatenate([wc[a, b] for a in range(3)], axis=0)))
        total = shift_columns(*parts, width) + bias[...]
        feats[start : start + size] = total.astype(BF16).reshape(size, width, chans)

        @pl.when(has_next)
        def _():
            moves[i].start()

        if i == 0:
            for copy in mats:
                copy.start()

    mean = head_mean(chans)

    def project(src, start, size, place):
        f = src[start : start + size].reshape(size * width, chans)
        blocked = (size, width, chans)
        keys[place : place + size] = normed(f, wk[...], gk[...], mean, 1).reshape(blocked)
        values[place : place + size] = dot(f, wv[...]).astype(BF16).reshape(blocked)

    lanes = GROUP * HD
    head = lax.broadcasted_iota(jnp.int32, (1, lanes), 1) // HD
    slot = lax.broadcasted_iota(jnp.int32, (1, KSRC * width), 1) // width
    base = band * rows - DISP - rows
    live = has_prev.astype(jnp.int32)

    def by_head(stacked):
        joined = stacked[0:width]
        for h in range(1, GROUP):
            joined = jnp.where(head == h, stacked[h * width : (h + 1) * width], joined)
        return joined

    def exponentials(n, cut, key):
        query = q[n, :, cut]
        stack = jnp.concatenate(
            [jnp.where(head == h, query, jnp.zeros_like(query)) for h in range(GROUP)], axis=0
        )
        return jnp.exp(
            lax.dot_general(stack, key, (((1,), (1,)), ((), ())), preferred_element_type=F32)
        )

    def own(n, carry):
        for g in range(chans // lanes):
            cut = pl.ds(g * lanes, lanes)
            expo = exponentials(n, cut, keys[n, :, cut])
            sums[n, g] = expo
            mixture[n, :, cut] = by_head(dot(expo.astype(BF16), values[n, :, cut]))
        return carry

    def block(n, carry):
        places = [
            jnp.clip(ids[0, j, n] - base, rows, 2 * rows + 2 * DISP - 1) for j in range(KSRC)
        ]
        mask = slot < valid[0, n] * live
        for g in range(chans // lanes):
            cut = pl.ds(g * lanes, lanes)
            key = jnp.concatenate([keys[p, :, cut] for p in places], axis=0)
            value = jnp.concatenate([values[p, :, cut] for p in places], axis=0)
            expo = jnp.where(mask, exponentials(n, cut, key), 0.0)
            folded = sums[n, g]
            for j in range(KSRC):
                folded = folded + expo[:, j * width : (j + 1) * width]
            inverse = 1.0 / jnp.sum(folded, axis=1, keepdims=True)
            part = by_head(dot(expo.astype(BF16), value)) + mixture[n, :, cut]
            mixed[n, :, cut] = (part * by_head(inverse)).astype(BF16)
        return carry

    for copy in mats:
        copy.wait()
    flat = feats[...].reshape(rows * width, chans)
    q[...] = normed(flat, wq[...], gq[...], mean, HD**-0.5).reshape(rows, width, chans)
    project(feats, 0, rows, 0)

    @pl.when(has_prev)
    def _():
        moves[0].wait_recv()

    @pl.when(has_prev & has_above)
    def _():
        relay_up.start()

    project(reach, DISP, DISP, rows + DISP)
    lax.fori_loop(0, rows, own, 0, unroll=True)

    @pl.when(has_prev)
    def _():
        moves[1].wait_recv()

    @pl.when(has_prev & has_below)
    def _():
        relay_down.start()

    project(reach, rows, DISP, 2 * rows)

    @pl.when(has_prev & has_above)
    def _():
        relay_down.wait_recv()

    project(reach, 0, DISP, rows)

    @pl.when(has_prev & has_below)
    def _():
        relay_up.wait_recv()

    project(reach, DISP + rows, DISP, 2 * rows + DISP)

    @pl.when(has_prev)
    def _():
        moves[2].wait_recv()

    project(reach, 2 * DISP, rows - 2 * DISP, rows + 2 * DISP)

    lax.fori_loop(0, rows, block, 0, unroll=True)
    flat = mixed[...].reshape(rows * width, chans)
    f = feats[...].reshape(rows * width, chans).astype(F32)
    out[...] = (f + dot(flat, wo[...])).astype(BF16).reshape(rows, width, chans)

    @pl.when(has_above)
    def _():
        halo_up.wait_send()

    @pl.when(has_below)
    def _():
        halo_down.wait_send()

    for copy in moves:

        @pl.when(has_next)
        def _():
            copy.wait_send()

    @pl.when(has_prev & has_above)
    def _():
        relay_up.wait_send()

    @pl.when(has_prev & has_below)
    def _():
        relay_down.wait_send()


VM = pl.BlockSpec(memory_space=pltpu.VMEM)
SM = pl.BlockSpec(memory_space=pltpu.SMEM)
ANY = pl.BlockSpec(memory_space=pl.ANY)


def shards(x, wc, bias, wq, wk, wv, wo, gq, gk, source_ids, valid_counts):
    x = x[0]
    rows, width, chans = x.shape
    square = pltpu.VMEM((chans, chans), BF16)

    def stack(count):
        return pltpu.VMEM((count, width, chans), BF16)

    out = pl.pallas_call(
        kernel,
        out_shape=jax.ShapeDtypeStruct((rows, width, chans), BF16),
        in_specs=[SM, SM] + [ANY] * 6 + [VM] * 3,
        out_specs=VM,
        scratch_shapes=[
            stack(rows + 2),
            pltpu.VMEM(wc.shape, BF16),
            square,
            square,
            square,
            square,
            stack(rows),
            stack(rows + 2 * DISP),
            stack(rows),
            stack(2 * rows + 2 * DISP),
            stack(2 * rows + 2 * DISP),
            stack(rows),
            pltpu.VMEM((rows, width, chans), F32),
            pltpu.VMEM((rows, chans // (GROUP * HD), GROUP * width, width), F32),
            pltpu.SemaphoreType.DMA((8,)),
            pltpu.SemaphoreType.DMA((7,)),
            pltpu.SemaphoreType.DMA((7,)),
        ],
        compiler_params=pltpu.CompilerParams(
            vmem_limit_bytes=56 * 2**20, collective_id=0, has_side_effects=True
        ),
    )(jnp.swapaxes(source_ids, 1, 2), valid_counts, x, wc, wq, wk, wv, wo, bias[None], gq[None], gk[None])
    return out[None]


def solution(mesh):
    return jax.shard_map(
        shards,
        mesh=mesh,
        in_specs=(P("frame", "row", None, None),)
        + (P(),) * 8
        + (P("frame", "row", None), P("frame", "row")),
        out_specs=P("frame", "row", None, None),
        check_vma=False,
    )
```
